32 devices in a mesh: tensor: 4 (over z), example: 8 (over y, x, core).
Axes of the slice: x: 2, y: 2, z: 4, core: 2. Of those that a mesh axis runs over, the one named last changes fastest.
Arguments:
- queries: bfloat16 [1, 4096, 4096], P(None, 'example', 'tensor'), may hold values from -0.0014648438 to 0.0014648438
- basis_out: bfloat16 [4096, 4096], P('example', 'tensor'), may hold values from -0.09375 to 0.09375
- basis_in: bfloat16 [4096, 4096], P('tensor', 'example'), may hold values from -0.09375 to 0.09375
- eigvals: float32 [4096, 4096], P('tensor', 'example'), may hold values from 0.25 to 4
- input_fac: bfloat16 [128, 8, 4096], P('example', None, 'tensor'), may hold values from -6 to 6
- grad_fac: bfloat16 [128, 8, 4096], P('example', None, 'tensor'), may hold values from -6 to 6
- cand_slot: int32 [128], replicated, may hold values from 0 to 127, as said below
- score_list: int32 [8, 16], replicated, may hold values from 0 to 127, as said below
- token_count: int32 [128], replicated, may hold values from 1 to 8
Outputs:
- scores: float32 [1, 128, 8], P(None, 'example')
The draws below stay inside these ranges and needn't reach their ends.
Inputs may be any that keep to these rules, and one draw needn't show every extreme that they name: `cand_slot`: a permutation; slot s belongs to owner s // 16. `score_list`: every candidate appears exactly once; a scorer's list holds at most 4 candidates of any one owner, and some scorer takes exactly 4 from some owner.
All inputs are finite; a program needn't handle non-finite values.
Results may differ from the reference program's by a relative error of at most 0.019.
Values may be sent and summed in bfloat16 or wider, within the bound.
A program may use at most 128 MiB of HBM per device.

```python
import math
import jax
import jax.numpy as jnp
from jax import lax

D = 4096
QUERIES = 1
CAND_DEV = 16
LEN = 8
CANDIDATES = 128
N_TENSOR = 4
N_EXAMPLE = 8


def routing_tables(key):
    base_key = jax.random.fold_in(key, 11)
    key_order, key_target, key_other, key_tie, key_perm = jax.random.split(base_key, 5)
    per_pair = CAND_DEV // N_EXAMPLE
    slot_ids = jnp.arange(CAND_DEV, dtype=jnp.int32)
    destination = jnp.tile((slot_ids // per_pair)[None, :], (N_EXAMPLE, 1))
    owner_order = jax.random.permutation(key_order, N_EXAMPLE)
    half_count = N_EXAMPLE // 2
    first_owners = owner_order[:half_count]
    second_owners = owner_order[half_count:2 * half_count]
    target_one = jax.random.randint(key_target, (half_count,), 0, N_EXAMPLE).astype(jnp.int32)
    target_two = ((target_one + 1 + jax.random.randint(key_other, (half_count,), 0, N_EXAMPLE - 1)) % N_EXAMPLE).astype(jnp.int32)
    rows_first = destination[first_owners]
    rows_first = jnp.where(rows_first == target_two[:, None], target_one[:, None], rows_first)
    rows_second = destination[second_owners]
    rows_second = jnp.where(rows_second == target_one[:, None], target_two[:, None], rows_second)
    destination = destination.at[first_owners].set(rows_first).at[second_owners].set(rows_second)
    total_slots = CAND_DEV * N_EXAMPLE
    tie_break = jax.random.permutation(key_tie, total_slots).astype(jnp.int32)
    sort_key = destination.reshape(-1).astype(jnp.int32) * total_slots + tie_break
    sorted_slots = jnp.argsort(sort_key, stable=True).astype(jnp.int32)
    slot_of_cand = jax.random.permutation(key_perm, total_slots).astype(jnp.int32)
    cand_of_slot = jnp.argsort(slot_of_cand, stable=True).astype(jnp.int32)
    lists = cand_of_slot[sorted_slots].reshape(N_EXAMPLE, CAND_DEV)
    return (slot_of_cand, lists)


def draw_cand_slot(key, part):
    slot_of_cand, lists = routing_tables(key)
    return slot_of_cand


def draw_score_list(key, part):
    slot_of_cand, lists = routing_tables(key)
    return lists


def draw_token_count(key, part):
    key_count, key_full = jax.random.split(jax.random.fold_in(key, 23))
    counts = jax.random.randint(key_count, (CAND_DEV * N_EXAMPLE,), 1, LEN + 1).astype(jnp.int32)
    full_index = jax.random.randint(key_full, (), 0, CAND_DEV * N_EXAMPLE)
    return counts.at[full_index].set(LEN).astype(jnp.int32)


def levels(stream_key, dims, cuts, low, top_value):
    def one(position, parts):
        draws = jax.random.uniform(jax.random.fold_in(jax.random.fold_in(stream_key, 6), position), (parts,), jnp.float32, low / len(cuts), top_value / len(cuts))
        return jnp.repeat(jnp.exp(draws), dims[position] // parts).reshape((-1,) + (1,) * (len(dims) - position - 1))

    loudness = one(*cuts[0])
    for cut in cuts[1:]:
        loudness = loudness * one(*cut)
    return loudness


def scatter_about(own_key, dims, deviation, bound, cuts=(), held_as=jnp.bfloat16):
    result = deviation * jax.random.normal(own_key, dims, jnp.float32)
    if cuts:
        result = result * levels(own_key, dims, cuts, -0.22, 0.18)
    return jnp.clip(result, -bound, bound).astype(held_as)


def setup_inputs(seed: int = 0) -> dict:
    key_list = jax.random.split(jax.random.key(seed), 10)
    queries = scatter_about(key_list[0], (QUERIES, D, D), (D * D) ** -0.5, 0.0014648438, ((1, 8), (2, 4)))
    basis_out = scatter_about(key_list[1], (D, D), D ** -0.5, 0.09375, ((0, 8), (1, 4)))
    basis_in = scatter_about(key_list[2], (D, D), D ** -0.5, 0.09375, ((0, 4), (1, 8)))
    eigvals = jnp.clip(jnp.exp(math.log(4.0) - 2.7725887 * jax.random.uniform(key_list[3], (D, D), jnp.float32) ** levels(key_list[3], (D, D), ((0, 4), (1, 8)), -0.2, 0.2)), 0.25, 4.0)
    input_fac = scatter_about(key_list[4], (CANDIDATES, LEN, D), 1.0, 6.0, ((0, 8), (2, 4)))
    grad_fac = scatter_about(key_list[5], (CANDIDATES, LEN, D), 1.0, 6.0, ((0, 8), (2, 4)))
    cand_slot = draw_cand_slot(jax.random.fold_in(key_list[9], 71), 0)
    score_list = draw_score_list(jax.random.fold_in(key_list[9], 71), 0)
    token_count = draw_token_count(jax.random.fold_in(key_list[9], 71), 0)
    return dict(queries=queries, basis_out=basis_out, basis_in=basis_in, eigvals=eigvals, input_fac=input_fac, grad_fac=grad_fac, cand_slot=cand_slot, score_list=score_list, token_count=token_count)


def reference(queries, basis_out, basis_in, eigvals, input_fac, grad_fac, cand_slot, score_list, token_count):
    out_block = D // N_EXAMPLE
    in_block = D // N_TENSOR

    def rotate_one(gradient):
        def out_step(running, block_index):
            rows_basis = lax.dynamic_slice_in_dim(basis_out, block_index * out_block, out_block, 0)
            rows_grad = lax.dynamic_slice_in_dim(gradient, block_index * out_block, out_block, 0)
            block_term = jnp.dot(rows_basis.T, rows_grad, preferred_element_type=jnp.float32).astype(jnp.bfloat16)
            block_term = lax.optimization_barrier(block_term)
            return running + block_term.astype(jnp.float32), None

        mixed_sum, _ = lax.scan(out_step, jnp.zeros((D, D), jnp.float32), jnp.arange(N_EXAMPLE, dtype=jnp.int32))
        rotated = mixed_sum.astype(jnp.bfloat16)

        def in_step(running, block_index):
            cols_rot = lax.dynamic_slice_in_dim(rotated, block_index * in_block, in_block, 1)
            rows_basis = lax.dynamic_slice_in_dim(basis_in, block_index * in_block, in_block, 0)
            block_term = jnp.dot(cols_rot, rows_basis, preferred_element_type=jnp.float32).astype(jnp.bfloat16)
            block_term = lax.optimization_barrier(block_term)
            return running + block_term.astype(jnp.float32), None

        core_sum, _ = lax.scan(in_step, jnp.zeros((D, D), jnp.float32), jnp.arange(N_TENSOR, dtype=jnp.int32))
        scaled = (core_sum / eigvals.T).astype(jnp.bfloat16)
        turned = jnp.dot(basis_out, scaled, preferred_element_type=jnp.float32).astype(jnp.bfloat16)
        return jnp.dot(turned, basis_in.T, preferred_element_type=jnp.float32).astype(jnp.bfloat16)

    precond = lax.map(rotate_one, queries)

    def score_one(candidate):
        cand_place = cand_slot[candidate]
        cand_acts = lax.dynamic_index_in_dim(input_fac, cand_place, 0, keepdims=False)
        cand_grads = lax.dynamic_index_in_dim(grad_fac, cand_place, 0, keepdims=False)
        weighted = jnp.stack([jnp.dot(cand_grads, precond[query_index], preferred_element_type=jnp.float32) for query_index in range(QUERIES)])
        token_scores = jnp.sum(cand_acts.astype(jnp.float32)[None] * weighted, axis=2)
        live_mask = jnp.arange(LEN, dtype=jnp.int32) < token_count[candidate]
        return jnp.where(live_mask[None], token_scores, jnp.float32(0.0))

    scored = lax.map(score_one, score_list.reshape(-1))
    return jnp.transpose(scored, (1, 0, 2))
```

```python
import jax
import jax.numpy as jnp
from jax import lax
from jax.sharding import PartitionSpec as P

BF = jnp.bfloat16
F32 = jnp.float32


def regroup_grads(grads, n_tensor, n_example):
    ratio = n_example // n_tensor
    half = grads.shape[1] // ratio
    parity = lax.axis_index("example") % ratio
    received = []
    for shift in range(ratio):
        piece = lax.dynamic_slice_in_dim(grads, ((parity + shift) % ratio) * half, half, 1)
        perm = []
        for t in range(n_tensor):
            for e in range(n_example):
                target = (e // ratio) * n_example + ratio * t + (e + shift) % ratio
                perm.append((t * n_example + e, target))
        received.append(lax.ppermute(piece, ("tensor", "example"), perm))
    stacked = jnp.stack(received)
    order = (parity - jnp.arange(ratio)) % ratio
    pieces = [lax.dynamic_index_in_dim(stacked, order[p], 0, keepdims=False) for p in range(ratio)]
    return jnp.concatenate(pieces, axis=0)


def body(
    queries, basis_out, basis_in, eigvals, input_fac, grad_fac, cand_slot, score_list, token_count
):
    n_example = lax.axis_size("example")
    n_tensor = lax.axis_size("tensor")
    my_index = lax.axis_index("example")
    cand_total = cand_slot.shape[0]
    token_len = input_fac.shape[1]
    list_len = score_list.shape[1]
    query_total, rows, width = queries.shape
    acts = input_fac.reshape(-1, width)
    grads = grad_fac.reshape(-1, width)
    tokens = acts.shape[0]

    in_rows = lax.all_gather(basis_in, "example", axis=1, tiled=True)
    moved_grads = regroup_grads(grads, n_tensor, n_example)
    out_rows = lax.all_gather(basis_out, "tensor", axis=1, tiled=True)
    left = jnp.concatenate([queries.reshape(-1, width), acts], axis=0)
    half_rotated = lax.psum_scatter(
        jnp.einsum("jl,rj->lr", in_rows, left, preferred_element_type=F32).astype(BF),
        "tensor",
        scatter_dimension=0,
        tiled=True,
    )
    split = query_total * rows
    acts_rot = lax.all_gather(half_rotated[:, split:], "example", axis=0)
    parts = [half_rotated[:, q * rows : (q + 1) * rows] for q in range(query_total)]
    right = jnp.concatenate(parts + [moved_grads], axis=0)
    core = lax.psum_scatter(
        jnp.einsum("ik,xi->kx", out_rows, right, preferred_element_type=F32).astype(BF),
        "example",
        scatter_dimension=0,
        tiled=True,
    )
    wide = half_rotated.shape[0]
    grads_rot = lax.all_gather(core[:, query_total * wide :], "tensor", axis=0)
    acts_flat = jnp.transpose(acts_rot, (1, 0, 2)).reshape(wide, -1).astype(F32)
    grads_flat = jnp.transpose(grads_rot, (1, 0, 2)).reshape(core.shape[0], -1)
    partial = []
    for q in range(query_total):
        scaled = (core[:, q * wide : (q + 1) * wide].astype(F32) / eigvals.T).astype(BF)
        weighted = jnp.einsum("kl,kt->lt", scaled, grads_flat, preferred_element_type=F32)
        partial.append(jnp.sum(weighted * acts_flat, axis=0))
    summed = lax.psum(jnp.stack(partial), ("tensor", "example"))
    by_slot = summed.reshape(query_total, cand_total, token_len)

    my_list = lax.dynamic_index_in_dim(score_list, my_index, 0, keepdims=False)
    ids = jnp.arange(cand_total, dtype=jnp.int32)
    matches = my_list[:, None] == ids[None, :]
    my_slot = jnp.sum(jnp.where(matches, cand_slot[None, :], 0), axis=1)
    my_count = jnp.sum(jnp.where(matches, token_count[None, :], 0), axis=1)
    pick = my_slot[:, None] == ids[None, :]
    scores = jnp.sum(jnp.where(pick[None, :, :, None], by_slot[:, None], F32(0.0)), axis=2)
    live = jnp.arange(token_len, dtype=jnp.int32)[None, :] < my_count[:, None]
    return jnp.where(live[None], scores, F32(0.0))


def solution(mesh):
    in_specs = (
        P(None, "example", "tensor"),
        P("example", "tensor"),
        P("tensor", "example"),
        P("tensor", "example"),
        P("example", None, "tensor"),
        P("example", None, "tensor"),
        P(),
        P(),
        P(),
    )
    out_specs = P(None, "example", None)
    return jax.shard_map(body, mesh=mesh, in_specs=in_specs, out_specs=out_specs, check_vma=False)
```

```python
import functools

import jax
import jax.numpy as jnp
from jax import lax
from jax.experimental import pallas as pl
from jax.experimental.pallas import tpu as pltpu
from jax.sharding import PartitionSpec as P

BF = jnp.bfloat16
F32 = jnp.float32
MESH = pl.DeviceIdType.MESH
VMEM_LIMIT = 56 * 1024 * 1024


def flip(index, bit):
    size = 1 << bit
    return index + size * (1 - 2 * ((index // size) % 2))


def flip_mask(index, mask, bits):
    for bit in range(bits):
        if (mask >> bit) & 1:
            index = flip(index, bit)
    return index


def remote(src, dst, send, recv, **where):
    return pltpu.make_async_remote_copy(
        src_ref=src, dst_ref=dst, send_sem=send, recv_sem=recv, device_id=where, device_id_type=MESH
    )


def greet_partners(me, bits):
    barrier = pltpu.get_barrier_semaphore()
    for bit in range(bits):
        pl.semaphore_signal(barrier, inc=1, device_id={"example": flip(me, bit)}, device_id_type=MESH)
    pl.semaphore_wait(barrier, bits)


def level_of(mask, order):
    for place, bit in enumerate(order):
        if (mask >> bit) & 1:
            return place
    return len(order)


def last_level(mask, order):
    return max(place for place, bit in enumerate(order) if (mask >> bit) & 1)


def gather_kernel(bits, x_ref, out_ref, send_sem, recv_sem, local_sem):
    me = lax.axis_index("example")
    half = x_ref.shape[0] // 2
    own = pltpu.make_async_copy(x_ref, out_ref.at[me], local_sem)
    own.start()
    greet_partners(me, bits)
    upper = list(range(1, bits))
    orders = [upper + [0], upper[::-1] + [0]]
    started = []

    def view(h, mask):
        return out_ref.at[flip_mask(me, mask, bits), pl.ds(h * half, half)]

    def send(h, mask, bit):
        src = x_ref.at[pl.ds(h * half, half)] if mask == 0 else view(h, mask)
        slot = mask | (1 << bit)
        copy = remote(src, view(h, mask), send_sem.at[h, slot], recv_sem.at[h, slot], example=flip(me, bit))
        copy.start()
        started.append(copy)

    def received(h, mask):
        remote(view(h, mask), view(h, mask), send_sem.at[h, mask], recv_sem.at[h, mask],
               example=flip(me, 0)).wait_recv()

    for place in range(bits):
        for h in range(2):
            send(h, 0, orders[h][place])
    arrivals = sorted(
        ((last_level(mask, orders[h]), bin(mask).count("1"), mask, h) for h in range(2) for mask in range(1, 1 << bits)),
        key=lambda item: (item[0], item[1], item[3], item[2]),
    )
    for place, _, mask, h in arrivals:
        received(h, mask)
        for bit in orders[h][place + 1 :]:
            send(h, mask, bit)
    for copy in started:
        copy.wait_send()
    own.wait()


def gather_blocks(x, n_example):
    bits = n_example.bit_length() - 1
    return pl.pallas_call(
        functools.partial(gather_kernel, bits),
        out_shape=jax.ShapeDtypeStruct((n_example,) + x.shape, x.dtype),
        in_specs=[pl.BlockSpec(memory_space=pl.ANY)],
        out_specs=pl.BlockSpec(memory_space=pl.ANY),
        scratch_shapes=[
            pltpu.SemaphoreType.DMA((2, n_example)),
            pltpu.SemaphoreType.DMA((2, n_example)),
            pltpu.SemaphoreType.DMA,
        ],
        compiler_params=pltpu.CompilerParams(collective_id=1, has_side_effects=True),
        cost_estimate=pl.CostEstimate(flops=0, bytes_accessed=100_000_000, transcendentals=0),
        name="gather_in_rows",
    )(x)


def line_kernel(n, ratio, left_ref, basis_ref, out_ref, held, inbox, send_sem, recv_sem):
    t = lax.axis_index("tensor")
    width = basis_ref.shape[2]
    barrier = pltpu.get_barrier_semaphore()

    @pl.when(t > 0)
    def _():
        pl.semaphore_signal(barrier, inc=1, device_id={"tensor": t - 1}, device_id_type=MESH)

    @pl.when(t < n - 1)
    def _():
        pl.semaphore_signal(barrier, inc=1, device_id={"tensor": t + 1}, device_id_type=MESH)

    pl.semaphore_wait(barrier, (t + n - 1) // n + (2 * n - 2 - t) // n)

    def product(block):
        return jnp.dot(left_ref[...], basis_ref[block], preferred_element_type=F32)

    def copy(way, block, partner):
        return remote(held.at[block], inbox.at[way, block], send_sem.at[block], recv_sem.at[way, block], tensor=partner)

    late = (2 * t) // n

    def unit(v, carry):
        u = v // 2
        way = (v % 2 + late) % 2
        up = (n - 1 - u // ratio) * ratio + u % ratio
        block = up + way * (u - up)
        d = block // ratio
        sign = 1 - 2 * way
        place = t + way * (n - 1 - 2 * t)
        goal = d + way * (n - 1 - 2 * d)

        @pl.when(place < goal)
        def _():
            held[block] = product(block).astype(BF)

            @pl.when(place > 0)
            def _():
                copy(way, block, t + sign).wait_recv()
                held[block] = (held[block].astype(F32) + inbox[way, block].astype(F32)).astype(BF)

            copy(way, block, t + sign).start()

        return carry

    lax.fori_loop(0, 2 * n * ratio, unit, 0)
    for sub in range(ratio):
        block = t * ratio + sub
        columns = pl.ds(sub * width, width)
        held[block] = product(block).astype(BF)

        @pl.when(t > 0)
        def _():
            copy(0, block, t - 1).wait_recv()
            held[block] = (held[block].astype(F32) + inbox[0, block].astype(F32)).astype(BF)

        @pl.when(t < n - 1)
        def _():
            copy(1, block, t + 1).wait_recv()
            held[block] = (held[block].astype(F32) + inbox[1, block].astype(F32)).astype(BF)

        out_ref[:, columns] = held[block]

    def drain(block, carry):
        d = block // ratio

        @pl.when(d > t)
        def _():
            copy(0, block, t + 1).wait_send()

        @pl.when(d < t)
        def _():
            copy(1, block, t - 1).wait_send()

        return carry

    lax.fori_loop(0, n * ratio, drain, 0)


def line_product(left, blocks, n):
    count, _, width = blocks.shape
    rows = left.shape[0]
    ratio = count // n
    return pl.pallas_call(
        functools.partial(line_kernel, n, ratio),
        out_shape=jax.ShapeDtypeStruct((rows, ratio * width), BF),
        in_specs=[pl.BlockSpec(memory_space=pltpu.VMEM)] * 2,
        out_specs=pl.BlockSpec(memory_space=pltpu.VMEM),
        scratch_shapes=[
            pltpu.VMEM((count, rows, width), BF),
            pltpu.VMEM((2, count, rows, width), BF),
            pltpu.SemaphoreType.DMA((count,)),
            pltpu.SemaphoreType.DMA((2, count)),
        ],
        compiler_params=pltpu.CompilerParams(
            collective_id=2, has_side_effects=True, vmem_limit_bytes=VMEM_LIMIT
        ),
        cost_estimate=pl.CostEstimate(flops=0, bytes_accessed=250_000_000, transcendentals=0),
        name="line_product",
    )(left, blocks)


def halving_kernel(bits, tile, left_ref, basis_ref, out_ref, held, inbox, send_sem, recv_sem):
    me = lax.axis_index("example")
    count = 1 << bits
    half = left_ref.shape[0] // 2
    width = held.shape[3]
    per_block = basis_ref.shape[2] // width
    greet_partners(me, bits)
    upper = list(range(1, bits))
    orders = [[0] + upper, [0] + upper[::-1]]

    def copy(h, mask, place):
        bit = orders[h][place]
        kept = mask & ~(1 << bit)
        where = slots[h][(place, kept)]
        return remote(held.at[h, mask], inbox.at[h, where], send_sem.at[h, mask], recv_sem.at[h, where],
                      example=flip(me, bit))

    slots = []
    for h in range(2):
        table = {}
        for place in range(bits):
            for mask in range(count):
                if level_of(mask, orders[h]) > place:
                    table[(place, mask)] = len(table)
        slots.append(table)

    def priority(mask, order):
        key = []
        for place, bit in enumerate(order):
            key.append(0 if (mask >> bit) & 1 else 1)
        return key

    started = []
    units = sorted(
        ((h, mask) for h in range(2) for mask in range(count)),
        key=lambda item: (priority(item[1], orders[item[0]]), item[0]),
    )
    for h, mask in units:
        level = level_of(mask, orders[h])
        for place in range(level):
            copy(h, mask | (1 << orders[h][place]), place).wait_recv()
        owner = flip_mask(me, mask, bits)
        columns = pl.ds(pl.multiple_of((owner % per_block) * width, width), width)
        inboxes = [slots[h][(place, mask)] for place in range(level)]

        def rows_of(step, carry):
            rows = pl.ds(pl.multiple_of(step * tile, tile), tile)
            source = pl.ds(pl.multiple_of(h * half + step * tile, tile), tile)
            total = jnp.dot(
                left_ref[source, :], basis_ref[owner // per_block, :, columns], preferred_element_type=F32
            )
            total = total.astype(BF).astype(F32)
            for where in inboxes:
                total += inbox[h, where, rows, :].astype(F32)
            if mask == 0:
                out_ref[source, :] = total.astype(BF)
            else:
                held[h, mask, rows, :] = total.astype(BF)
            return carry

        lax.fori_loop(0, half // tile, rows_of, 0)
        if mask:
            sent = copy(h, mask, level)
            sent.start()
            started.append(sent)
    for sent in started:
        sent.wait_send()


def halving_product(left, blocks, n_example):
    bits = n_example.bit_length() - 1
    rows = left.shape[0]
    width = blocks.shape[0] * blocks.shape[2] // n_example
    half = rows // 2
    tile = 128
    while half % tile:
        tile //= 2
    return pl.pallas_call(
        functools.partial(halving_kernel, bits, tile),
        out_shape=jax.ShapeDtypeStruct((rows, width), BF),
        in_specs=[pl.BlockSpec(memory_space=pltpu.VMEM)] * 2,
        out_specs=pl.BlockSpec(memory_space=pltpu.VMEM),
        scratch_shapes=[
            pltpu.VMEM((2, n_example, half, width), BF),
            pltpu.VMEM((2, n_example - 1, half, width), BF),
            pltpu.SemaphoreType.DMA((2, n_example)),
            pltpu.SemaphoreType.DMA((2, n_example)),
        ],
        compiler_params=pltpu.CompilerParams(
            collective_id=3, has_side_effects=True, vmem_limit_bytes=VMEM_LIMIT
        ),
        cost_estimate=pl.CostEstimate(flops=0, bytes_accessed=150_000_000, transcendentals=0),
        name="halving_product",
    )(left, blocks)


def total_kernel(steps, x_ref, out_ref, held, inbox, send_sem, recv_sem):
    barrier = pltpu.get_barrier_semaphore()
    where = [{axis: flip(lax.axis_index(axis), bit)} for axis, bit in steps]
    for target in where:
        pl.semaphore_signal(barrier, inc=1, device_id=target, device_id_type=MESH)
    pl.semaphore_wait(barrier, len(steps))
    held[0] = x_ref[...]
    for k, target in enumerate(where):
        copy = remote(held.at[k], inbox.at[k], send_sem.at[k], recv_sem.at[k], **target)
        copy.start()
        copy.wait()
        if k + 1 < len(steps):
            held[k + 1] = held[k] + inbox[k]
        else:
            out_ref[...] = held[k] + inbox[k]


def total_over_devices(x, n_tensor, n_example):
    steps = [("example", bit) for bit in range(n_example.bit_length() - 1)]
    steps += [("tensor", bit) for bit in range(n_tensor.bit_length() - 1)]
    flat = x.reshape(-1, 128)
    return pl.pallas_call(
        functools.partial(total_kernel, steps),
        out_shape=jax.ShapeDtypeStruct(flat.shape, F32),
        in_specs=[pl.BlockSpec(memory_space=pltpu.VMEM)],
        out_specs=pl.BlockSpec(memory_space=pltpu.VMEM),
        scratch_shapes=[
            pltpu.VMEM((len(steps),) + flat.shape, F32),
            pltpu.VMEM((len(steps),) + flat.shape, F32),
            pltpu.SemaphoreType.DMA((len(steps),)),
            pltpu.SemaphoreType.DMA((len(steps),)),
        ],
        compiler_params=pltpu.CompilerParams(collective_id=4, has_side_effects=True),
        name="total_scores",
    )(flat).reshape(x.shape)


def regroup_grads(grads, n_tensor, n_example):
    ratio = n_example // n_tensor
    half = grads.shape[1] // ratio
    parity = lax.axis_index("example") % ratio
    received = []
    for shift in range(ratio):
        piece = lax.dynamic_slice_in_dim(grads, ((parity + shift) % ratio) * half, half, 1)
        perm = []
        for t in range(n_tensor):
            for e in range(n_example):
                target = (e // ratio) * n_example + ratio * t + (e + shift) % ratio
                perm.append((t * n_example + e, target))
        received.append(lax.ppermute(piece, ("tensor", "example"), perm))
    stacked = jnp.stack(received)
    order = (parity - jnp.arange(ratio)) % ratio
    pieces = [lax.dynamic_index_in_dim(stacked, order[p], 0, keepdims=False) for p in range(ratio)]
    return jnp.concatenate(pieces, axis=0)


def body(
    queries, basis_out, basis_in, eigvals, input_fac, grad_fac, cand_slot, score_list, token_count
):
    n_example = lax.axis_size("example")
    n_tensor = lax.axis_size("tensor")
    my_index = lax.axis_index("example")
    cand_total = cand_slot.shape[0]
    token_len = input_fac.shape[1]
    list_len = score_list.shape[1]
    query_total, rows, width = queries.shape
    acts = input_fac.reshape(-1, width)
    grads = grad_fac.reshape(-1, width)
    tokens = acts.shape[0]

    moved_grads = regroup_grads(grads, n_tensor, n_example)
    out_rows = lax.all_gather(basis_out, "tensor", axis=0)
    in_rows = gather_blocks(basis_in, n_example)
    left = jnp.concatenate([queries.reshape(-1, width), acts], axis=0)
    half_rotated = line_product(left, in_rows, n_tensor)
    split = query_total * rows
    acts_rot = lax.all_gather(half_rotated[split:], "example", axis=0, tiled=True)
    parts = [half_rotated[q * rows : (q + 1) * rows].T for q in range(query_total)]
    right = jnp.concatenate(parts + [moved_grads], axis=0)
    core = halving_product(right, out_rows, n_example)
    wide = half_rotated.shape[1]
    grads_rot = lax.all_gather(core[query_total * wide :], "tensor", axis=0, tiled=True)
    partial = []
    for q in range(query_total):
        scaled = (core[q * wide : (q + 1) * wide].astype(F32) / eigvals).astype(BF)
        weighted = jnp.einsum("tk,lk->tl", grads_rot, scaled, preferred_element_type=F32)
        partial.append(jnp.sum(weighted * acts_rot.astype(F32), axis=1))
    summed = total_over_devices(jnp.stack(partial), n_tensor, n_example)
    by_slot = summed.reshape(query_total, cand_total, token_len)

    my_list = lax.dynamic_index_in_dim(score_list, my_index, 0, keepdims=False)
    ids = jnp.arange(cand_total, dtype=jnp.int32)
    matches = my_list[:, None] == ids[None, :]
    my_slot = jnp.sum(jnp.where(matches, cand_slot[None, :], 0), axis=1)
    my_count = jnp.sum(jnp.where(matches, token_count[None, :], 0), axis=1)
    pick = my_slot[:, None] == ids[None, :]
    scores = jnp.sum(jnp.where(pick[None, :, :, None], by_slot[:, None], F32(0.0)), axis=2)
    live = jnp.arange(token_len, dtype=jnp.int32)[None, :] < my_count[:, None]
    return jnp.where(live[None], scores, F32(0.0))


def solution(mesh):
    in_specs = (
        P(None, "example", "tensor"),
        P("example", "tensor"),
        P("tensor", "example"),
        P("tensor", "example"),
        P("example", None, "tensor"),
        P("example", None, "tensor"),
        P(),
        P(),
        P(),
    )
    out_specs = P(None, "example", None)
    return jax.shard_map(body, mesh=mesh, in_specs=in_specs, out_specs=out_specs, check_vma=False)
```

```python
import functools

import jax
import jax.numpy as jnp
from jax import lax
from jax.experimental import pallas as pl
from jax.experimental.pallas import tpu as pltpu
from jax.sharding import PartitionSpec as P

BF = jnp.bfloat16
F32 = jnp.float32
MESH = pl.DeviceIdType.MESH
VMEM_LIMIT = 56 * 1024 * 1024


def flip(index, bit):
    size = 1 << bit
    return index + size * (1 - 2 * ((index // size) % 2))


def flip_mask(index, mask, bits):
    for bit in range(bits):
        if (mask >> bit) & 1:
            index = flip(index, bit)
    return index


def remote(src, dst, send, recv, **where):
    return pltpu.make_async_remote_copy(
        src_ref=src, dst_ref=dst, send_sem=send, recv_sem=recv, device_id=where, device_id_type=MESH
    )


def greet_partners(me, bits):
    barrier = pltpu.get_barrier_semaphore()
    for bit in range(bits):
        pl.semaphore_signal(barrier, inc=1, device_id={"example": flip(me, bit)}, device_id_type=MESH)
    pl.semaphore_wait(barrier, bits)


def level_of(mask, order):
    for place, bit in enumerate(order):
        if (mask >> bit) & 1:
            return place
    return len(order)


def last_level(mask, order):
    return max(place for place, bit in enumerate(order) if (mask >> bit) & 1)


def gather_kernel(bits, x_ref, out_ref, send_sem, recv_sem, local_sem):
    me = lax.axis_index("example")
    half = x_ref.shape[0] // 2
    own = pltpu.make_async_copy(x_ref, out_ref.at[me], local_sem)
    own.start()
    greet_partners(me, bits)
    upper = list(range(1, bits))
    orders = [upper + [0], upper[::-1] + [0]]
    started = []

    def view(h, mask):
        return out_ref.at[flip_mask(me, mask, bits), pl.ds(h * half, half)]

    def send(h, mask, bit):
        src = x_ref.at[pl.ds(h * half, half)] if mask == 0 else view(h, mask)
        slot = mask | (1 << bit)
        copy = remote(src, view(h, mask), send_sem.at[h, slot], recv_sem.at[h, slot], example=flip(me, bit))
        copy.start()
        started.append(copy)

    def received(h, mask):
        remote(view(h, mask), view(h, mask), send_sem.at[h, mask], recv_sem.at[h, mask],
               example=flip(me, 0)).wait_recv()

    for place in range(bits):
        for h in range(2):
            send(h, 0, orders[h][place])
    arrivals = sorted(
        ((last_level(mask, orders[h]), bin(mask).count("1"), mask, h) for h in range(2) for mask in range(1, 1 << bits)),
        key=lambda item: (item[0], item[1], item[3], item[2]),
    )
    for place, _, mask, h in arrivals:
        received(h, mask)
        for bit in orders[h][place + 1 :]:
            send(h, mask, bit)
    for copy in started:
        copy.wait_send()
    own.wait()


def gather_blocks(x, n_example):
    bits = n_example.bit_length() - 1
    return pl.pallas_call(
        functools.partial(gather_kernel, bits),
        out_shape=jax.ShapeDtypeStruct((n_example,) + x.shape, x.dtype),
        in_specs=[pl.BlockSpec(memory_space=pl.ANY)],
        out_specs=pl.BlockSpec(memory_space=pl.ANY),
        scratch_shapes=[
            pltpu.SemaphoreType.DMA((2, n_example)),
            pltpu.SemaphoreType.DMA((2, n_example)),
            pltpu.SemaphoreType.DMA,
        ],
        compiler_params=pltpu.CompilerParams(collective_id=1, has_side_effects=True),
        cost_estimate=pl.CostEstimate(flops=0, bytes_accessed=100_000_000, transcendentals=0),
        name="gather_in_rows",
    )(x)


def line_kernel(n, ratio, left_ref, basis_ref, out_ref, held, inbox, send_sem, recv_sem):
    t = lax.axis_index("tensor")
    width = basis_ref.shape[2]
    barrier = pltpu.get_barrier_semaphore()

    @pl.when(t > 0)
    def _():
        pl.semaphore_signal(barrier, inc=1, device_id={"tensor": t - 1}, device_id_type=MESH)

    @pl.when(t < n - 1)
    def _():
        pl.semaphore_signal(barrier, inc=1, device_id={"tensor": t + 1}, device_id_type=MESH)

    pl.semaphore_wait(barrier, (t + n - 1) // n + (2 * n - 2 - t) // n)

    def product(block):
        return jnp.dot(left_ref[...], basis_ref[block], preferred_element_type=F32)

    def copy(way, block, partner):
        return remote(held.at[block], inbox.at[way, block], send_sem.at[block], recv_sem.at[way, block], tensor=partner)

    late = (2 * t) // n

    def unit(v, carry):
        u = v // 2
        way = (v % 2 + late) % 2
        up = (n - 1 - u // ratio) * ratio + u % ratio
        block = up + way * (u - up)
        d = block // ratio
        sign = 1 - 2 * way
        place = t + way * (n - 1 - 2 * t)
        goal = d + way * (n - 1 - 2 * d)

        @pl.when(place < goal)
        def _():
            held[block] = product(block).astype(BF)

            @pl.when(place > 0)
            def _():
                copy(way, block, t + sign).wait_recv()
                held[block] = (held[block].astype(F32) + inbox[way, block].astype(F32)).astype(BF)

            @pl.when(u >= 2)
            def _():
                before = u - 2
                before_up = (n - 1 - before // ratio) * ratio + before % ratio
                copy(way, before_up + way * (before - before_up), t + sign).wait_send()

            copy(way, block, t + sign).start()

        return carry

    lax.fori_loop(0, 2 * n * ratio, unit, 0)
    for sub in range(ratio):
        block = t * ratio + sub
        columns = pl.ds(sub * width, width)
        held[block] = product(block).astype(BF)

        @pl.when(t > 0)
        def _():
            copy(0, block, t - 1).wait_recv()
            held[block] = (held[block].astype(F32) + inbox[0, block].astype(F32)).astype(BF)

        @pl.when(t < n - 1)
        def _():
            copy(1, block, t + 1).wait_recv()
            held[block] = (held[block].astype(F32) + inbox[1, block].astype(F32)).astype(BF)

        out_ref[:, columns] = held[block]

    def drain(k, carry):
        @pl.when(t < n - 1)
        def _():
            last = (n - 1 - t) * ratio - 1 - k
            copy(0, (n - 1 - last // ratio) * ratio + last % ratio, t + 1).wait_send()

        @pl.when(t > 0)
        def _():
            copy(1, t * ratio - 1 - k, t - 1).wait_send()

        return carry

    lax.fori_loop(0, 2, drain, 0)


def line_product(left, blocks, n):
    count, _, width = blocks.shape
    rows = left.shape[0]
    ratio = count // n
    return pl.pallas_call(
        functools.partial(line_kernel, n, ratio),
        out_shape=jax.ShapeDtypeStruct((rows, ratio * width), BF),
        in_specs=[pl.BlockSpec(memory_space=pltpu.VMEM)] * 2,
        out_specs=pl.BlockSpec(memory_space=pltpu.VMEM),
        scratch_shapes=[
            pltpu.VMEM((count, rows, width), BF),
            pltpu.VMEM((2, count, rows, width), BF),
            pltpu.SemaphoreType.DMA((count,)),
            pltpu.SemaphoreType.DMA((2, count)),
        ],
        compiler_params=pltpu.CompilerParams(
            collective_id=2, has_side_effects=True, vmem_limit_bytes=VMEM_LIMIT
        ),
        cost_estimate=pl.CostEstimate(flops=0, bytes_accessed=250_000_000, transcendentals=0),
        name="line_product",
    )(left, blocks)


def unit_order(bits, orders, parts):
    masks = range(1 << bits)

    def chunk(pair, keep):
        found = [(p, mask) for p in pair for mask in masks if keep(mask, orders[p])]

        def key(item):
            order = orders[item[0]]
            return ([0 if (item[1] >> bit) & 1 else 1 for bit in order], item[0])

        return sorted(found, key=key)

    def at_level(level):
        return lambda mask, order: level_of(mask, order) == level

    def first_then(level):
        return lambda mask, order: level_of(mask, order) == 0 and level_of(mask & ~1, order) == level

    small = [chunk(parts[:2], at_level(level)) for level in range(bits + 1)]
    large = []
    for level in range(1, bits + 1):
        large.append(chunk(parts[2:], first_then(level)))
        large.append(chunk(parts[2:], at_level(level)))
    units = []
    for place in range(max(len(small), len(large))):
        for chunks in (small, large):
            if place < len(chunks):
                units += chunks[place]
    return units


def halving_kernel(bits, n_tensor, core_rows, left_ref, basis_ref, core_ref, grads_ref, held, inbox, send_sem, recv_sem, out_sem, in_sem):
    me = lax.axis_index("example")
    t = lax.axis_index("tensor")
    count = 1 << bits
    width = held.shape[2]
    per_block = basis_ref.shape[2] // width
    grad_rows = left_ref.shape[0] - core_rows
    spans = [
        (core_rows, grad_rows // 2),
        (core_rows + grad_rows // 2, grad_rows // 2),
        (0, core_rows // 2),
        (core_rows // 2, core_rows // 2),
    ]
    upper = list(range(1, bits))
    orders = [[0] + upper, [0] + upper[::-1]] * 2
    peers = [(t + k) % n_tensor for k in range(1, n_tensor)]
    barrier = pltpu.get_barrier_semaphore()
    for bit in range(bits):
        pl.semaphore_signal(barrier, inc=1, device_id={"example": flip(me, bit)}, device_id_type=MESH)
    for peer in peers:
        pl.semaphore_signal(barrier, inc=1, device_id={"tensor": peer}, device_id_type=MESH)
    pl.semaphore_wait(barrier, bits + n_tensor - 1)

    slots = []
    for p in range(4):
        table = {}
        for place in range(bits):
            for mask in range(count):
                if level_of(mask, orders[p]) > place:
                    table[(place, mask)] = len(table)
        slots.append(table)

    def copy(p, mask, place):
        bit = orders[p][place]
        where = slots[p][(place, mask & ~(1 << bit))]
        rows = pl.ds(*spans[p])
        return remote(held.at[mask, rows], inbox.at[where, rows], send_sem.at[p, mask], recv_sem.at[p, where],
                      example=flip(me, bit))

    def spread(k):
        rows = grads_ref.at[t]
        return remote(rows, rows, out_sem.at[k], in_sem.at[k], tensor=peers[k])

    started = []
    finished = 0
    for p, mask in unit_order(bits, orders, [0, 1, 2, 3]):
        level = level_of(mask, orders[p])
        for place in range(level):
            copy(p, mask | (1 << orders[p][place]), place).wait_recv()
        owner = flip_mask(me, mask, bits)
        columns = pl.ds(pl.multiple_of((owner % per_block) * width, width), width)
        inboxes = [slots[p][(place, mask)] for place in range(level)]
        start, size = spans[p]
        tile = 128
        while size % tile:
            tile //= 2

        def rows_of(step, carry):
            rows = pl.ds(pl.multiple_of(start + step * tile, tile), tile)
            total = jnp.dot(
                left_ref[rows, :], basis_ref[owner // per_block, :, columns], preferred_element_type=F32
            )
            total = total.astype(BF).astype(F32)
            for where in inboxes:
                total += inbox[where, rows, :].astype(F32)
            if mask:
                held[mask, rows, :] = total.astype(BF)
            elif p >= 2:
                core_ref[rows, :] = total.astype(BF)
            else:
                grads_ref[t, pl.ds(pl.multiple_of(start - core_rows + step * tile, tile), tile), :] = total.astype(BF)
            return carry

        lax.fori_loop(0, size // tile, rows_of, 0)
        if mask:
            sent = copy(p, mask, level)
            sent.start()
            started.append(sent)
        elif p < 2:
            finished += 1
            if finished == 2:
                for k in range(n_tensor - 1):
                    spread(k).start()
    for sent in started:
        sent.wait_send()
    for k in range(n_tensor - 1):
        spread(k).wait_send()
        source = grads_ref.at[(t - 1 - k + n_tensor) % n_tensor]
        remote(source, source, out_sem.at[k], in_sem.at[k], tensor=peers[k]).wait_recv()


def halving_product(left, blocks, n_example, core_rows):
    bits = n_example.bit_length() - 1
    rows = left.shape[0]
    n_tensor = blocks.shape[0]
    width = n_tensor * blocks.shape[2] // n_example
    vmem = pl.BlockSpec(memory_space=pltpu.VMEM)
    return pl.pallas_call(
        functools.partial(halving_kernel, bits, n_tensor, core_rows),
        out_shape=(
            jax.ShapeDtypeStruct((core_rows, width), BF),
            jax.ShapeDtypeStruct((n_tensor, rows - core_rows, width), BF),
        ),
        in_specs=[vmem, vmem],
        out_specs=(vmem, vmem),
        scratch_shapes=[
            pltpu.VMEM((n_example, rows, width), BF),
            pltpu.VMEM((n_example - 1, rows, width), BF),
            pltpu.SemaphoreType.DMA((4, n_example)),
            pltpu.SemaphoreType.DMA((4, n_example)),
            pltpu.SemaphoreType.DMA((n_tensor - 1,)),
            pltpu.SemaphoreType.DMA((n_tensor - 1,)),
        ],
        compiler_params=pltpu.CompilerParams(
            collective_id=3, has_side_effects=True, vmem_limit_bytes=VMEM_LIMIT
        ),
        cost_estimate=pl.CostEstimate(flops=0, bytes_accessed=150_000_000, transcendentals=0),
        name="halving_product",
    )(left, blocks)


def total_kernel(steps, x_ref, out_ref, held, inbox, send_sem, recv_sem):
    barrier = pltpu.get_barrier_semaphore()
    where = [{axis: flip(lax.axis_index(axis), bit)} for axis, bit in steps]
    for target in where:
        pl.semaphore_signal(barrier, inc=1, device_id=target, device_id_type=MESH)
    pl.semaphore_wait(barrier, len(steps))
    held[0] = x_ref[...]
    for k, target in enumerate(where):
        copy = remote(held.at[k], inbox.at[k], send_sem.at[k], recv_sem.at[k], **target)
        copy.start()
        copy.wait()
        if k + 1 < len(steps):
            held[k + 1] = held[k] + inbox[k]
        else:
            out_ref[...] = held[k] + inbox[k]


def total_over_devices(x, n_tensor, n_example):
    steps = [("example", bit) for bit in range(n_example.bit_length() - 1)]
    steps += [("tensor", bit) for bit in range(n_tensor.bit_length() - 1)]
    flat = x.reshape(-1, 128)
    return pl.pallas_call(
        functools.partial(total_kernel, steps),
        out_shape=jax.ShapeDtypeStruct(flat.shape, F32),
        in_specs=[pl.BlockSpec(memory_space=pltpu.VMEM)],
        out_specs=pl.BlockSpec(memory_space=pltpu.VMEM),
        scratch_shapes=[
            pltpu.VMEM((len(steps),) + flat.shape, F32),
            pltpu.VMEM((len(steps),) + flat.shape, F32),
            pltpu.SemaphoreType.DMA((len(steps),)),
            pltpu.SemaphoreType.DMA((len(steps),)),
        ],
        compiler_params=pltpu.CompilerParams(collective_id=4, has_side_effects=True),
        name="total_scores",
    )(flat).reshape(x.shape)


def regroup_grads(grads, n_tensor, n_example):
    ratio = n_example // n_tensor
    half = grads.shape[1] // ratio
    parity = lax.axis_index("example") % ratio
    received = []
    for shift in range(ratio):
        piece = lax.dynamic_slice_in_dim(grads, ((parity + shift) % ratio) * half, half, 1)
        perm = []
        for t in range(n_tensor):
            for e in range(n_example):
                target = (e // ratio) * n_example + ratio * t + (e + shift) % ratio
                perm.append((t * n_example + e, target))
        received.append(lax.ppermute(piece, ("tensor", "example"), perm))
    stacked = jnp.stack(received)
    order = (parity - jnp.arange(ratio)) % ratio
    pieces = [lax.dynamic_index_in_dim(stacked, order[p], 0, keepdims=False) for p in range(ratio)]
    return jnp.concatenate(pieces, axis=0)


def body(
    queries, basis_out, basis_in, eigvals, input_fac, grad_fac, cand_slot, score_list, token_count
):
    n_example = lax.axis_size("example")
    n_tensor = lax.axis_size("tensor")
    my_index = lax.axis_index("example")
    cand_total = cand_slot.shape[0]
    token_len = input_fac.shape[1]
    list_len = score_list.shape[1]
    query_total, rows, width = queries.shape
    acts = input_fac.reshape(-1, width)
    grads = grad_fac.reshape(-1, width)
    tokens = acts.shape[0]

    moved_grads = regroup_grads(grads, n_tensor, n_example)
    out_rows = lax.all_gather(basis_out, "tensor", axis=0)
    in_rows = gather_blocks(basis_in, n_example)
    left = jnp.concatenate([queries.reshape(-1, width), acts], axis=0)
    half_rotated = line_product(left, in_rows, n_tensor)
    split = query_total * rows
    acts_rot = lax.all_gather(half_rotated[split:], "example", axis=0, tiled=True)
    parts = [half_rotated[q * rows : (q + 1) * rows].T for q in range(query_total)]
    right = jnp.concatenate(parts + [moved_grads], axis=0)
    wide = half_rotated.shape[1]
    core, grads_rot = halving_product(right, out_rows, n_example, query_total * wide)
    grads_rot = grads_rot.reshape(-1, core.shape[1])
    partial = []
    for q in range(query_total):
        scaled = (core[q * wide : (q + 1) * wide].astype(F32) / eigvals).astype(BF)
        weighted = jnp.einsum("tk,lk->tl", grads_rot, scaled, preferred_element_type=F32)
        partial.append(jnp.sum(weighted * acts_rot.astype(F32), axis=1))
    summed = total_over_devices(jnp.stack(partial), n_tensor, n_example)
    by_slot = summed.reshape(query_total, cand_total, token_len)

    my_list = lax.dynamic_index_in_dim(score_list, my_index, 0, keepdims=False)
    ids = jnp.arange(cand_total, dtype=jnp.int32)
    matches = my_list[:, None] == ids[None, :]
    my_slot = jnp.sum(jnp.where(matches, cand_slot[None, :], 0), axis=1)
    my_count = jnp.sum(jnp.where(matches, token_count[None, :], 0), axis=1)
    pick = my_slot[:, None] == ids[None, :]
    scores = jnp.sum(jnp.where(pick[None, :, :, None], by_slot[:, None], F32(0.0)), axis=2)
    live = jnp.arange(token_len, dtype=jnp.int32)[None, :] < my_count[:, None]
    return jnp.where(live[None], scores, F32(0.0))


def solution(mesh):
    in_specs = (
        P(None, "example", "tensor"),
        P("example", "tensor"),
        P("tensor", "example"),
        P("tensor", "example"),
        P("example", None, "tensor"),
        P("example", None, "tensor"),
        P(),
        P(),
        P(),
    )
    out_specs = P(None, "example", None)
    return jax.shard_map(body, mesh=mesh, in_specs=in_specs, out_specs=out_specs, check_vma=False)
```

```python
import functools

import jax
import jax.numpy as jnp
from jax import lax
from jax.experimental import pallas as pl
from jax.experimental.pallas import tpu as pltpu
from jax.sharding import PartitionSpec as P

BF = jnp.bfloat16
F32 = jnp.float32
MESH = pl.DeviceIdType.MESH
VMEM_LIMIT = 56 * 1024 * 1024


def flip(index, bit):
    size = 1 << bit
    return index + size * (1 - 2 * ((index // size) % 2))


def flip_mask(index, mask, bits):
    for bit in range(bits):
        if (mask >> bit) & 1:
            index = flip(index, bit)
    return index


def remote(src, dst, send, recv, **where):
    return pltpu.make_async_remote_copy(
        src_ref=src, dst_ref=dst, send_sem=send, recv_sem=recv, device_id=where, device_id_type=MESH
    )


def greet_partners(me, bits):
    barrier = pltpu.get_barrier_semaphore()
    for bit in range(bits):
        pl.semaphore_signal(barrier, inc=1, device_id={"example": flip(me, bit)}, device_id_type=MESH)
    pl.semaphore_wait(barrier, bits)


def level_of(mask, order):
    for place, bit in enumerate(order):
        if (mask >> bit) & 1:
            return place
    return len(order)


def last_level(mask, order):
    return max(place for place, bit in enumerate(order) if (mask >> bit) & 1)


def line_neighbours(t, n):
    return (t + n - 1) // n + (2 * n - 2 - t) // n


def greet_line(barrier, t, n):
    @pl.when(t > 0)
    def _():
        pl.semaphore_signal(barrier, inc=1, device_id={"tensor": t - 1}, device_id_type=MESH)

    @pl.when(t < n - 1)
    def _():
        pl.semaphore_signal(barrier, inc=1, device_id={"tensor": t + 1}, device_id_type=MESH)


def spread_line(t, n, rows_ref, first, size, parts, send_sem, recv_sem):
    step = size // parts

    def copy(way, block, part, partner):
        rows = rows_ref.at[block, pl.ds(first + part * step, step)]
        return remote(rows, rows, send_sem.at[way, block, part], recv_sem.at[block, part], tensor=partner)

    def begin():
        for part in range(parts):
            @pl.when(t < n - 1)
            def _():
                copy(0, t, part, t + 1).start()

            @pl.when(t > 0)
            def _():
                copy(1, t, part, t - 1).start()

    def relay(far):
        for part in range(parts):
            @pl.when(t >= far)
            def _():
                copy(0, t - far, part, t - 1).wait_recv()

                @pl.when(t < n - 1)
                def _():
                    copy(0, t - far, part, t + 1).start()

            @pl.when(t + far < n)
            def _():
                copy(1, t + far, part, t + 1).wait_recv()

                @pl.when(t > 0)
                def _():
                    copy(1, t + far, part, t - 1).start()

    def finish():
        for block in range(n):
            for part in range(parts):
                @pl.when((t >= block) & (t < n - 1))
                def _():
                    copy(0, block, part, t + 1).wait_send()

                @pl.when((t <= block) & (t > 0))
                def _():
                    copy(1, block, part, t - 1).wait_send()

    return begin, relay, finish


def gather_kernel(bits, n, early, x_ref, y_ref, out_ref, line_ref, send_sem, recv_sem, local_sem, up_sem, down_sem):
    me = lax.axis_index("example")
    half = x_ref.shape[0] // 2
    own = pltpu.make_async_copy(x_ref, out_ref.at[me], local_sem.at[0])
    own.start()
    t = lax.axis_index("tensor")
    mine = pltpu.make_async_copy(y_ref, line_ref.at[t], local_sem.at[1])
    mine.start()
    barrier = pltpu.get_barrier_semaphore()
    for bit in range(bits):
        pl.semaphore_signal(barrier, inc=1, device_id={"example": flip(me, bit)}, device_id_type=MESH)
    greet_line(barrier, t, n)
    pl.semaphore_wait(barrier, bits + line_neighbours(t, n))
    upper = list(range(1, bits))
    orders = [upper + [0], upper[::-1] + [0]]
    started = []

    def view(h, mask):
        return out_ref.at[flip_mask(me, mask, bits), pl.ds(h * half, half)]

    def send(h, mask, bit):
        src = x_ref.at[pl.ds(h * half, half)] if mask == 0 else view(h, mask)
        slot = mask | (1 << bit)
        copy = remote(src, view(h, mask), send_sem.at[h, slot], recv_sem.at[h, slot], example=flip(me, bit))
        copy.start()
        started.append(copy)

    def received(h, mask):
        remote(view(h, mask), view(h, mask), send_sem.at[h, mask], recv_sem.at[h, mask],
               example=flip(me, 0)).wait_recv()

    for place in range(bits):
        for h in range(2):
            send(h, 0, orders[h][place])
    mine.wait()
    begin, relay, finish = spread_line(t, n, line_ref, 0, early, 2, up_sem, down_sem)
    begin()
    arrivals = sorted(
        ((last_level(mask, orders[h]), bin(mask).count("1"), mask, h) for h in range(2) for mask in range(1, 1 << bits)),
        key=lambda item: (item[0], item[1], item[3], item[2]),
    )
    turns = [item[0] for item in arrivals]
    far = 0
    for turn, (place, _, mask, h) in enumerate(arrivals):
        if turn and turns[turn - 1] != place and far + 1 < n:
            far += 1
            relay(far)
        received(h, mask)
        for bit in orders[h][place + 1 :]:
            send(h, mask, bit)
    while far + 1 < n:
        far += 1
        relay(far)
    for copy in started:
        copy.wait_send()
    finish()
    own.wait()


def gather_blocks(x, y, n_example, n_tensor, early):
    bits = n_example.bit_length() - 1
    anywhere = pl.BlockSpec(memory_space=pl.ANY)
    return pl.pallas_call(
        functools.partial(gather_kernel, bits, n_tensor, early),
        out_shape=(
            jax.ShapeDtypeStruct((n_example,) + x.shape, x.dtype),
            jax.ShapeDtypeStruct((n_tensor,) + y.shape, y.dtype),
        ),
        in_specs=[anywhere] * 2,
        out_specs=(anywhere,) * 2,
        scratch_shapes=[
            pltpu.SemaphoreType.DMA((2, n_example)),
            pltpu.SemaphoreType.DMA((2, n_example)),
            pltpu.SemaphoreType.DMA((2,)),
            pltpu.SemaphoreType.DMA((2, n_tensor, 2)),
            pltpu.SemaphoreType.DMA((n_tensor, 2)),
        ],
        compiler_params=pltpu.CompilerParams(collective_id=1, has_side_effects=True),
        cost_estimate=pl.CostEstimate(flops=0, bytes_accessed=100_000_000, transcendentals=0),
        name="gather_rows",
    )(x, y)


def line_kernel(n, ratio, early, left_ref, basis_ref, _, out_ref, line_ref, held, inbox, send_sem, recv_sem, up_sem, down_sem):
    t = lax.axis_index("tensor")
    width = basis_ref.shape[2]
    barrier = pltpu.get_barrier_semaphore()
    greet_line(barrier, t, n)
    pl.semaphore_wait(barrier, line_neighbours(t, n))
    rest = line_ref.shape[1] - early
    begin, relay, finish = spread_line(t, n, line_ref, early, rest, 1, up_sem, down_sem)
    begin()

    def product(block):
        return jnp.dot(left_ref[...], basis_ref[block], preferred_element_type=F32)

    def copy(way, block, partner):
        return remote(held.at[block], inbox.at[way, block], send_sem.at[block], recv_sem.at[way, block], tensor=partner)

    late = (2 * t) // n

    def unit(v, carry):
        u = v // 2

        @pl.when((v > 0) & (v % (2 * ratio) == 0))
        def _():
            relay(v // (2 * ratio))

        way = (v % 2 + late) % 2
        up = (n - 1 - u // ratio) * ratio + u % ratio
        block = up + way * (u - up)
        d = block // ratio
        sign = 1 - 2 * way
        place = t + way * (n - 1 - 2 * t)
        goal = d + way * (n - 1 - 2 * d)

        @pl.when(place < goal)
        def _():
            held[block] = product(block).astype(BF)

            @pl.when(place > 0)
            def _():
                copy(way, block, t + sign).wait_recv()
                held[block] = (held[block].astype(F32) + inbox[way, block].astype(F32)).astype(BF)

            @pl.when(u >= 2)
            def _():
                before = u - 2
                before_up = (n - 1 - before // ratio) * ratio + before % ratio
                copy(way, before_up + way * (before - before_up), t + sign).wait_send()

            copy(way, block, t + sign).start()

        return carry

    lax.fori_loop(0, 2 * n * ratio, unit, 0)
    for sub in range(ratio):
        block = t * ratio + sub
        columns = pl.ds(sub * width, width)
        held[block] = product(block).astype(BF)

        @pl.when(t > 0)
        def _():
            copy(0, block, t - 1).wait_recv()
            held[block] = (held[block].astype(F32) + inbox[0, block].astype(F32)).astype(BF)

        @pl.when(t < n - 1)
        def _():
            copy(1, block, t + 1).wait_recv()
            held[block] = (held[block].astype(F32) + inbox[1, block].astype(F32)).astype(BF)

        out_ref[:, columns] = held[block]

    def drain(k, carry):
        @pl.when(t < n - 1)
        def _():
            last = (n - 1 - t) * ratio - 1 - k
            copy(0, (n - 1 - last // ratio) * ratio + last % ratio, t + 1).wait_send()

        @pl.when(t > 0)
        def _():
            copy(1, t * ratio - 1 - k, t - 1).wait_send()

        return carry

    lax.fori_loop(0, 2, drain, 0)
    finish()


def line_product(left, blocks, out_rows, n, early):
    count, _, width = blocks.shape
    rows = left.shape[0]
    ratio = count // n
    vmem = pl.BlockSpec(memory_space=pltpu.VMEM)
    anywhere = pl.BlockSpec(memory_space=pl.ANY)
    return pl.pallas_call(
        functools.partial(line_kernel, n, ratio, early),
        out_shape=(
            jax.ShapeDtypeStruct((rows, ratio * width), BF),
            jax.ShapeDtypeStruct(out_rows.shape, out_rows.dtype),
        ),
        in_specs=[vmem, vmem, anywhere],
        out_specs=(vmem, anywhere),
        input_output_aliases={2: 1},
        scratch_shapes=[
            pltpu.VMEM((count, rows, width), BF),
            pltpu.VMEM((2, count, rows, width), BF),
            pltpu.SemaphoreType.DMA((count,)),
            pltpu.SemaphoreType.DMA((2, count)),
            pltpu.SemaphoreType.DMA((2, n, 1)),
            pltpu.SemaphoreType.DMA((n, 1)),
        ],
        compiler_params=pltpu.CompilerParams(
            collective_id=2, has_side_effects=True, vmem_limit_bytes=VMEM_LIMIT
        ),
        cost_estimate=pl.CostEstimate(flops=0, bytes_accessed=250_000_000, transcendentals=0),
        name="line_product",
    )(left, blocks, out_rows)


def unit_order(bits, orders, parts):
    masks = range(1 << bits)

    def chunk(pair, keep):
        found = [(p, mask) for p in pair for mask in masks if keep(mask, orders[p])]

        def key(item):
            order = orders[item[0]]
            return ([0 if (item[1] >> bit) & 1 else 1 for bit in order], item[0])

        return sorted(found, key=key)

    def at_level(level):
        return lambda mask, order: level_of(mask, order) == level

    def first_then(level):
        return lambda mask, order: level_of(mask, order) == 0 and level_of(mask & ~1, order) == level

    small = [chunk(parts[:2], at_level(level)) for level in range(bits + 1)]
    large = []
    for level in range(1, bits + 1):
        large.append(chunk(parts[2:], first_then(level)))
        large.append(chunk(parts[2:], at_level(level)))
    units = []
    for place in range(max(len(small), len(large))):
        for chunks in (small, large):
            if place < len(chunks):
                units += chunks[place]
    return units


def halving_kernel(bits, n_tensor, core_rows, left_ref, basis_ref, core_ref, grads_ref, held, inbox, send_sem, recv_sem, out_sem, in_sem):
    me = lax.axis_index("example")
    t = lax.axis_index("tensor")
    count = 1 << bits
    width = held.shape[2]
    per_block = basis_ref.shape[2] // width
    grad_rows = left_ref.shape[0] - core_rows
    spans = [
        (core_rows, grad_rows // 2),
        (core_rows + grad_rows // 2, grad_rows // 2),
        (0, core_rows // 2),
        (core_rows // 2, core_rows // 2),
    ]
    upper = list(range(1, bits))
    orders = [[0] + upper, [0] + upper[::-1]] * 2
    peers = [(t + k) % n_tensor for k in range(1, n_tensor)]
    barrier = pltpu.get_barrier_semaphore()
    for bit in range(bits):
        pl.semaphore_signal(barrier, inc=1, device_id={"example": flip(me, bit)}, device_id_type=MESH)
    for peer in peers:
        pl.semaphore_signal(barrier, inc=1, device_id={"tensor": peer}, device_id_type=MESH)
    pl.semaphore_wait(barrier, bits + n_tensor - 1)

    slots = []
    for p in range(4):
        table = {}
        for place in range(bits):
            for mask in range(count):
                if level_of(mask, orders[p]) > place:
                    table[(place, mask)] = len(table)
        slots.append(table)

    def copy(p, mask, place):
        bit = orders[p][place]
        where = slots[p][(place, mask & ~(1 << bit))]
        rows = pl.ds(*spans[p])
        return remote(held.at[mask, rows], inbox.at[where, rows], send_sem.at[p, mask], recv_sem.at[p, where],
                      example=flip(me, bit))

    def spread(k):
        rows = grads_ref.at[t]
        return remote(rows, rows, out_sem.at[k], in_sem.at[k], tensor=peers[k])

    started = []
    finished = 0
    for p, mask in unit_order(bits, orders, [0, 1, 2, 3]):
        level = level_of(mask, orders[p])
        for place in range(level):
            copy(p, mask | (1 << orders[p][place]), place).wait_recv()
        owner = flip_mask(me, mask, bits)
        columns = pl.ds(pl.multiple_of((owner % per_block) * width, width), width)
        inboxes = [slots[p][(place, mask)] for place in range(level)]
        start, size = spans[p]
        tile = 128
        while size % tile:
            tile //= 2

        def rows_of(step, carry):
            rows = pl.ds(pl.multiple_of(start + step * tile, tile), tile)
            total = jnp.dot(
                left_ref[rows, :], basis_ref[owner // per_block, :, columns], preferred_element_type=F32
            )
            total = total.astype(BF).astype(F32)
            for where in inboxes:
                total += inbox[where, rows, :].astype(F32)
            if mask:
                held[mask, rows, :] = total.astype(BF)
            elif p >= 2:
                core_ref[rows, :] = total.astype(BF)
            else:
                grads_ref[t, pl.ds(pl.multiple_of(start - core_rows + step * tile, tile), tile), :] = total.astype(BF)
            return carry

        lax.fori_loop(0, size // tile, rows_of, 0)
        if mask:
            sent = copy(p, mask, level)
            sent.start()
            started.append(sent)
        elif p < 2:
            finished += 1
            if finished == 2:
                for k in range(n_tensor - 1):
                    spread(k).start()
    for sent in started:
        sent.wait_send()
    for k in range(n_tensor - 1):
        spread(k).wait_send()
        source = grads_ref.at[(t - 1 - k + n_tensor) % n_tensor]
        remote(source, source, out_sem.at[k], in_sem.at[k], tensor=peers[k]).wait_recv()


def halving_product(left, blocks, n_example, core_rows):
    bits = n_example.bit_length() - 1
    rows = left.shape[0]
    n_tensor = blocks.shape[0]
    width = n_tensor * blocks.shape[2] // n_example
    vmem = pl.BlockSpec(memory_space=pltpu.VMEM)
    return pl.pallas_call(
        functools.partial(halving_kernel, bits, n_tensor, core_rows),
        out_shape=(
            jax.ShapeDtypeStruct((core_rows, width), BF),
            jax.ShapeDtypeStruct((n_tensor, rows - core_rows, width), BF),
        ),
        in_specs=[vmem, vmem],
        out_specs=(vmem, vmem),
        scratch_shapes=[
            pltpu.VMEM((n_example, rows, width), BF),
            pltpu.VMEM((n_example - 1, rows, width), BF),
            pltpu.SemaphoreType.DMA((4, n_example)),
            pltpu.SemaphoreType.DMA((4, n_example)),
            pltpu.SemaphoreType.DMA((n_tensor - 1,)),
            pltpu.SemaphoreType.DMA((n_tensor - 1,)),
        ],
        compiler_params=pltpu.CompilerParams(
            collective_id=3, has_side_effects=True, vmem_limit_bytes=VMEM_LIMIT
        ),
        cost_estimate=pl.CostEstimate(flops=0, bytes_accessed=150_000_000, transcendentals=0),
        name="halving_product",
    )(left, blocks)


def total_kernel(steps, x_ref, out_ref, held, inbox, send_sem, recv_sem):
    barrier = pltpu.get_barrier_semaphore()
    where = [{axis: flip(lax.axis_index(axis), bit)} for axis, bit in steps]
    for target in where:
        pl.semaphore_signal(barrier, inc=1, device_id=target, device_id_type=MESH)
    pl.semaphore_wait(barrier, len(steps))
    held[0] = x_ref[...]
    for k, target in enumerate(where):
        copy = remote(held.at[k], inbox.at[k], send_sem.at[k], recv_sem.at[k], **target)
        copy.start()
        copy.wait()
        if k + 1 < len(steps):
            held[k + 1] = held[k] + inbox[k]
        else:
            out_ref[...] = held[k] + inbox[k]


def total_over_devices(x, n_tensor, n_example):
    steps = [("example", bit) for bit in range(n_example.bit_length() - 1)]
    steps += [("tensor", bit) for bit in range(n_tensor.bit_length() - 1)]
    flat = x.reshape(-1, 128)
    return pl.pallas_call(
        functools.partial(total_kernel, steps),
        out_shape=jax.ShapeDtypeStruct(flat.shape, F32),
        in_specs=[pl.BlockSpec(memory_space=pltpu.VMEM)],
        out_specs=pl.BlockSpec(memory_space=pltpu.VMEM),
        scratch_shapes=[
            pltpu.VMEM((len(steps),) + flat.shape, F32),
            pltpu.VMEM((len(steps),) + flat.shape, F32),
            pltpu.SemaphoreType.DMA((len(steps),)),
            pltpu.SemaphoreType.DMA((len(steps),)),
        ],
        compiler_params=pltpu.CompilerParams(collective_id=4, has_side_effects=True),
        name="total_scores",
    )(flat).reshape(x.shape)


def regroup_grads(grads, n_tensor, n_example):
    ratio = n_example // n_tensor
    half = grads.shape[1] // ratio
    parity = lax.axis_index("example") % ratio
    received = []
    for shift in range(ratio):
        piece = lax.dynamic_slice_in_dim(grads, ((parity + shift) % ratio) * half, half, 1)
        perm = []
        for t in range(n_tensor):
            for e in range(n_example):
                target = (e // ratio) * n_example + ratio * t + (e + shift) % ratio
                perm.append((t * n_example + e, target))
        received.append(lax.ppermute(piece, ("tensor", "example"), perm))
    stacked = jnp.stack(received)
    order = (parity - jnp.arange(ratio)) % ratio
    pieces = [lax.dynamic_index_in_dim(stacked, order[p], 0, keepdims=False) for p in range(ratio)]
    return jnp.concatenate(pieces, axis=0)


def body(
    queries, basis_out, basis_in, eigvals, input_fac, grad_fac, cand_slot, score_list, token_count
):
    n_example = lax.axis_size("example")
    n_tensor = lax.axis_size("tensor")
    my_index = lax.axis_index("example")
    cand_total = cand_slot.shape[0]
    token_len = input_fac.shape[1]
    list_len = score_list.shape[1]
    query_total, rows, width = queries.shape
    acts = input_fac.reshape(-1, width)
    grads = grad_fac.reshape(-1, width)
    tokens = acts.shape[0]

    moved_grads = regroup_grads(grads, n_tensor, n_example)
    early = basis_out.shape[0] * 5 // 8
    in_rows, out_rows = gather_blocks(basis_in, basis_out, n_example, n_tensor, early)
    left = jnp.concatenate([queries.reshape(-1, width), acts], axis=0)
    left, moved_grads = lax.optimization_barrier((left, moved_grads))
    half_rotated, out_rows = line_product(left, in_rows, out_rows, n_tensor, early)
    split = query_total * rows
    acts_rot = lax.all_gather(half_rotated[split:], "example", axis=0, tiled=True)
    parts = [half_rotated[q * rows : (q + 1) * rows].T for q in range(query_total)]
    right = jnp.concatenate(parts + [moved_grads], axis=0)
    wide = half_rotated.shape[1]
    core, grads_rot = halving_product(right, out_rows, n_example, query_total * wide)
    grads_rot = grads_rot.reshape(-1, core.shape[1])
    partial = []
    for q in range(query_total):
        scaled = (core[q * wide : (q + 1) * wide].astype(F32) / eigvals).astype(BF)
        weighted = jnp.einsum("tk,lk->tl", grads_rot, scaled, preferred_element_type=F32)
        partial.append(jnp.sum(weighted * acts_rot.astype(F32), axis=1))
    summed = total_over_devices(jnp.stack(partial), n_tensor, n_example)
    by_slot = summed.reshape(query_total, cand_total, token_len)

    my_list = lax.dynamic_index_in_dim(score_list, my_index, 0, keepdims=False)
    ids = jnp.arange(cand_total, dtype=jnp.int32)
    matches = my_list[:, None] == ids[None, :]
    my_slot = jnp.sum(jnp.where(matches, cand_slot[None, :], 0), axis=1)
    my_count = jnp.sum(jnp.where(matches, token_count[None, :], 0), axis=1)
    pick = my_slot[:, None] == ids[None, :]
    scores = jnp.sum(jnp.where(pick[None, :, :, None], by_slot[:, None], F32(0.0)), axis=2)
    live = jnp.arange(token_len, dtype=jnp.int32)[None, :] < my_count[:, None]
    return jnp.where(live[None], scores, F32(0.0))


def solution(mesh):
    in_specs = (
        P(None, "example", "tensor"),
        P("example", "tensor"),
        P("tensor", "example"),
        P("tensor", "example"),
        P("example", None, "tensor"),
        P("example", None, "tensor"),
        P(),
        P(),
        P(),
    )
    out_specs = P(None, "example", None)
    return jax.shard_map(body, mesh=mesh, in_specs=in_specs, out_specs=out_specs, check_vma=False)
```

```python
import functools

import jax
import jax.numpy as jnp
from jax import lax
from jax.experimental import pallas as pl
from jax.experimental.pallas import tpu as pltpu
from jax.sharding import PartitionSpec as P

BF = jnp.bfloat16
F32 = jnp.float32
MESH = pl.DeviceIdType.MESH
VMEM_LIMIT = 56 * 1024 * 1024


def flip(index, bit):
    size = 1 << bit
    return index + size * (1 - 2 * ((index // size) % 2))


def flip_mask(index, mask, bits):
    for bit in range(bits):
        if (mask >> bit) & 1:
            index = flip(index, bit)
    return index


def remote(src, dst, send, recv, **where):
    return pltpu.make_async_remote_copy(
        src_ref=src, dst_ref=dst, send_sem=send, recv_sem=recv, device_id=where, device_id_type=MESH
    )


def greet_partners(me, bits):
    barrier = pltpu.get_barrier_semaphore()
    for bit in range(bits):
        pl.semaphore_signal(barrier, inc=1, device_id={"example": flip(me, bit)}, device_id_type=MESH)
    pl.semaphore_wait(barrier, bits)


def level_of(mask, order):
    for place, bit in enumerate(order):
        if (mask >> bit) & 1:
            return place
    return len(order)


def last_level(mask, order):
    return max(place for place, bit in enumerate(order) if (mask >> bit) & 1)


def gather_kernel(bits, x_ref, out_ref, send_sem, recv_sem, local_sem):
    me = lax.axis_index("example")
    half = x_ref.shape[0] // 2
    own = pltpu.make_async_copy(x_ref, out_ref.at[me], local_sem)
    own.start()
    greet_partners(me, bits)
    upper = list(range(1, bits))
    orders = [upper + [0], upper[::-1] + [0]]
    started = []

    def view(h, mask):
        return out_ref.at[flip_mask(me, mask, bits), pl.ds(h * half, half)]

    def send(h, mask, bit):
        src = x_ref.at[pl.ds(h * half, half)] if mask == 0 else view(h, mask)
        slot = mask | (1 << bit)
        copy = remote(src, view(h, mask), send_sem.at[h, slot], recv_sem.at[h, slot], example=flip(me, bit))
        copy.start()
        started.append(copy)

    def received(h, mask):
        remote(view(h, mask), view(h, mask), send_sem.at[h, mask], recv_sem.at[h, mask],
               example=flip(me, 0)).wait_recv()

    for place in range(bits):
        for h in range(2):
            send(h, 0, orders[h][place])
    arrivals = sorted(
        ((last_level(mask, orders[h]), bin(mask).count("1"), mask, h) for h in range(2) for mask in range(1, 1 << bits)),
        key=lambda item: (item[0], item[1], item[3], item[2]),
    )
    for place, _, mask, h in arrivals:
        received(h, mask)
        for bit in orders[h][place + 1 :]:
            send(h, mask, bit)
    for copy in started:
        copy.wait_send()
    own.wait()


def gather_blocks(x, n_example):
    bits = n_example.bit_length() - 1
    return pl.pallas_call(
        functools.partial(gather_kernel, bits),
        out_shape=jax.ShapeDtypeStruct((n_example,) + x.shape, x.dtype),
        in_specs=[pl.BlockSpec(memory_space=pl.ANY)],
        out_specs=pl.BlockSpec(memory_space=pl.ANY),
        scratch_shapes=[
            pltpu.SemaphoreType.DMA((2, n_example)),
            pltpu.SemaphoreType.DMA((2, n_example)),
            pltpu.SemaphoreType.DMA,
        ],
        compiler_params=pltpu.CompilerParams(collective_id=1, has_side_effects=True),
        cost_estimate=pl.CostEstimate(flops=0, bytes_accessed=100_000_000, transcendentals=0),
        name="gather_in_rows",
    )(x)


def line_kernel(n, ratio, left_ref, basis_ref, out_ref, held, inbox, send_sem, recv_sem):
    t = lax.axis_index("tensor")
    width = basis_ref.shape[2]
    barrier = pltpu.get_barrier_semaphore()

    @pl.when(t > 0)
    def _():
        pl.semaphore_signal(barrier, inc=1, device_id={"tensor": t - 1}, device_id_type=MESH)

    @pl.when(t < n - 1)
    def _():
        pl.semaphore_signal(barrier, inc=1, device_id={"tensor": t + 1}, device_id_type=MESH)

    pl.semaphore_wait(barrier, (t + n - 1) // n + (2 * n - 2 - t) // n)

    def product(block):
        return jnp.dot(left_ref[...], basis_ref[block], preferred_element_type=F32)

    def copy(way, block, partner):
        return remote(held.at[block], inbox.at[way, block], send_sem.at[block], recv_sem.at[way, block], tensor=partner)

    late = (2 * t) // n

    def unit(v, carry):
        u = v // 2
        way = (v % 2 + late) % 2
        up = (n - 1 - u // ratio) * ratio + u % ratio
        block = up + way * (u - up)
        d = block // ratio
        sign = 1 - 2 * way
        place = t + way * (n - 1 - 2 * t)
        goal = d + way * (n - 1 - 2 * d)

        @pl.when(place < goal)
        def _():
            held[block] = product(block).astype(BF)

            @pl.when(place > 0)
            def _():
                copy(way, block, t + sign).wait_recv()
                held[block] = (held[block].astype(F32) + inbox[way, block].astype(F32)).astype(BF)

            @pl.when(u >= 2)
            def _():
                before = u - 2
                before_up = (n - 1 - before // ratio) * ratio + before % ratio
                copy(way, before_up + way * (before - before_up), t + sign).wait_send()

            copy(way, block, t + sign).start()

        return carry

    lax.fori_loop(0, 2 * n * ratio, unit, 0)
    for sub in range(ratio):
        block = t * ratio + sub
        columns = pl.ds(sub * width, width)
        held[block] = product(block).astype(BF)

        @pl.when(t > 0)
        def _():
            copy(0, block, t - 1).wait_recv()
            held[block] = (held[block].astype(F32) + inbox[0, block].astype(F32)).astype(BF)

        @pl.when(t < n - 1)
        def _():
            copy(1, block, t + 1).wait_recv()
            held[block] = (held[block].astype(F32) + inbox[1, block].astype(F32)).astype(BF)

        out_ref[:, columns] = held[block]

    def drain(k, carry):
        @pl.when(t < n - 1)
        def _():
            last = (n - 1 - t) * ratio - 1 - k
            copy(0, (n - 1 - last // ratio) * ratio + last % ratio, t + 1).wait_send()

        @pl.when(t > 0)
        def _():
            copy(1, t * ratio - 1 - k, t - 1).wait_send()

        return carry

    lax.fori_loop(0, 2, drain, 0)


def line_product(left, blocks, n):
    count, _, width = blocks.shape
    rows = left.shape[0]
    ratio = count // n
    return pl.pallas_call(
        functools.partial(line_kernel, n, ratio),
        out_shape=jax.ShapeDtypeStruct((rows, ratio * width), BF),
        in_specs=[pl.BlockSpec(memory_space=pltpu.VMEM)] * 2,
        out_specs=pl.BlockSpec(memory_space=pltpu.VMEM),
        scratch_shapes=[
            pltpu.VMEM((count, rows, width), BF),
            pltpu.VMEM((2, count, rows, width), BF),
            pltpu.SemaphoreType.DMA((count,)),
            pltpu.SemaphoreType.DMA((2, count)),
        ],
        compiler_params=pltpu.CompilerParams(
            collective_id=2, has_side_effects=True, vmem_limit_bytes=VMEM_LIMIT
        ),
        cost_estimate=pl.CostEstimate(flops=0, bytes_accessed=250_000_000, transcendentals=0),
        name="line_product",
    )(left, blocks)


def unit_order(bits, orders, parts):
    masks = range(1 << bits)

    def chunk(pair, keep):
        found = [(p, mask) for p in pair for mask in masks if keep(mask, orders[p])]

        def key(item):
            order = orders[item[0]]
            return ([0 if (item[1] >> bit) & 1 else 1 for bit in order], item[0])

        return sorted(found, key=key)

    def at_level(level):
        return lambda mask, order: level_of(mask, order) == level

    def first_then(level):
        return lambda mask, order: level_of(mask, order) == 0 and level_of(mask & ~1, order) == level

    small = [chunk(parts[:2], at_level(level)) for level in range(bits + 1)]
    large = []
    for level in range(1, bits + 1):
        large.append(chunk(parts[2:], first_then(level)))
        large.append(chunk(parts[2:], at_level(level)))
    units = []
    for place in range(max(len(small), len(large))):
        for chunks in (small, large):
            if place < len(chunks):
                units += chunks[place]
    return units


def halving_kernel(bits, n_tensor, core_rows, left_ref, basis_ref, core_ref, grads_ref, held, inbox, send_sem, recv_sem, out_sem, in_sem):
    me = lax.axis_index("example")
    t = lax.axis_index("tensor")
    count = 1 << bits
    width = held.shape[2]
    per_block = basis_ref.shape[2] // width
    grad_rows = left_ref.shape[0] - core_rows
    spans = [
        (core_rows, grad_rows // 2),
        (core_rows + grad_rows // 2, grad_rows // 2),
        (0, core_rows // 2),
        (core_rows // 2, core_rows // 2),
    ]
    upper = list(range(1, bits))
    orders = [[0] + upper, [0] + upper[::-1]] * 2
    peers = [(t + k) % n_tensor for k in range(1, n_tensor)]
    barrier = pltpu.get_barrier_semaphore()
    for bit in range(bits):
        pl.semaphore_signal(barrier, inc=1, device_id={"example": flip(me, bit)}, device_id_type=MESH)
    for peer in peers:
        pl.semaphore_signal(barrier, inc=1, device_id={"tensor": peer}, device_id_type=MESH)
    pl.semaphore_wait(barrier, bits + n_tensor - 1)

    slots = []
    for p in range(4):
        table = {}
        for place in range(bits):
            for mask in range(count):
                if level_of(mask, orders[p]) > place:
                    table[(place, mask)] = len(table)
        slots.append(table)

    def copy(p, mask, place):
        bit = orders[p][place]
        where = slots[p][(place, mask & ~(1 << bit))]
        rows = pl.ds(*spans[p])
        return remote(held.at[mask, rows], inbox.at[where, rows], send_sem.at[p, mask], recv_sem.at[p, where],
                      example=flip(me, bit))

    def spread(k):
        rows = grads_ref.at[t]
        return remote(rows, rows, out_sem.at[k], in_sem.at[k], tensor=peers[k])

    started = []
    finished = 0
    for p, mask in unit_order(bits, orders, [0, 1, 2, 3]):
        level = level_of(mask, orders[p])
        for place in range(level):
            copy(p, mask | (1 << orders[p][place]), place).wait_recv()
        owner = flip_mask(me, mask, bits)
        columns = pl.ds(pl.multiple_of((owner % per_block) * width, width), width)
        inboxes = [slots[p][(place, mask)] for place in range(level)]
        start, size = spans[p]
        tile = 128
        while size % tile:
            tile //= 2

        def rows_of(step, carry):
            rows = pl.ds(pl.multiple_of(start + step * tile, tile), tile)
            total = jnp.dot(
                left_ref[rows, :], basis_ref[owner // per_block, :, columns], preferred_element_type=F32
            )
            total = total.astype(BF).astype(F32)
            for where in inboxes:
                total += inbox[where, rows, :].astype(F32)
            if mask:
                held[mask, rows, :] = total.astype(BF)
            elif p >= 2:
                core_ref[rows, :] = total.astype(BF)
            else:
                grads_ref[t, pl.ds(pl.multiple_of(start - core_rows + step * tile, tile), tile), :] = total.astype(BF)
            return carry

        lax.fori_loop(0, size // tile, rows_of, 0)
        if mask:
            sent = copy(p, mask, level)
            sent.start()
            started.append(sent)
        elif p < 2:
            finished += 1
            if finished == 2:
                for k in range(n_tensor - 1):
                    spread(k).start()
    for sent in started:
        sent.wait_send()
    for k in range(n_tensor - 1):
        spread(k).wait_send()
        source = grads_ref.at[(t - 1 - k + n_tensor) % n_tensor]
        remote(source, source, out_sem.at[k], in_sem.at[k], tensor=peers[k]).wait_recv()


def halving_product(left, blocks, n_example, core_rows):
    bits = n_example.bit_length() - 1
    rows = left.shape[0]
    n_tensor = blocks.shape[0]
    width = n_tensor * blocks.shape[2] // n_example
    vmem = pl.BlockSpec(memory_space=pltpu.VMEM)
    return pl.pallas_call(
        functools.partial(halving_kernel, bits, n_tensor, core_rows),
        out_shape=(
            jax.ShapeDtypeStruct((core_rows, width), BF),
            jax.ShapeDtypeStruct((n_tensor, rows - core_rows, width), BF),
        ),
        in_specs=[vmem, vmem],
        out_specs=(vmem, vmem),
        scratch_shapes=[
            pltpu.VMEM((n_example, rows, width), BF),
            pltpu.VMEM((n_example - 1, rows, width), BF),
            pltpu.SemaphoreType.DMA((4, n_example)),
            pltpu.SemaphoreType.DMA((4, n_example)),
            pltpu.SemaphoreType.DMA((n_tensor - 1,)),
            pltpu.SemaphoreType.DMA((n_tensor - 1,)),
        ],
        compiler_params=pltpu.CompilerParams(
            collective_id=3, has_side_effects=True, vmem_limit_bytes=VMEM_LIMIT
        ),
        cost_estimate=pl.CostEstimate(flops=0, bytes_accessed=150_000_000, transcendentals=0),
        name="halving_product",
    )(left, blocks)


def total_kernel(steps, x_ref, out_ref, held, inbox, send_sem, recv_sem):
    barrier = pltpu.get_barrier_semaphore()
    where = [{axis: flip(lax.axis_index(axis), bit)} for axis, bit in steps]
    for target in where:
        pl.semaphore_signal(barrier, inc=1, device_id=target, device_id_type=MESH)
    pl.semaphore_wait(barrier, len(steps))
    held[0] = x_ref[...]
    for k, target in enumerate(where):
        copy = remote(held.at[k], inbox.at[k], send_sem.at[k], recv_sem.at[k], **target)
        copy.start()
        copy.wait()
        if k + 1 < len(steps):
            held[k + 1] = held[k] + inbox[k]
        else:
            out_ref[...] = held[k] + inbox[k]


def total_over_devices(x, n_tensor, n_example):
    steps = [("example", bit) for bit in range(n_example.bit_length() - 1)]
    steps += [("tensor", bit) for bit in range(n_tensor.bit_length() - 1)]
    flat = x.reshape(-1, 128)
    return pl.pallas_call(
        functools.partial(total_kernel, steps),
        out_shape=jax.ShapeDtypeStruct(flat.shape, F32),
        in_specs=[pl.BlockSpec(memory_space=pltpu.VMEM)],
        out_specs=pl.BlockSpec(memory_space=pltpu.VMEM),
        scratch_shapes=[
            pltpu.VMEM((len(steps),) + flat.shape, F32),
            pltpu.VMEM((len(steps),) + flat.shape, F32),
            pltpu.SemaphoreType.DMA((len(steps),)),
            pltpu.SemaphoreType.DMA((len(steps),)),
        ],
        compiler_params=pltpu.CompilerParams(collective_id=4, has_side_effects=True),
        name="total_scores",
    )(flat).reshape(x.shape)


def regroup_grads(grads, n_tensor, n_example):
    ratio = n_example // n_tensor
    half = grads.shape[1] // ratio
    parity = lax.axis_index("example") % ratio
    received = []
    for shift in range(ratio):
        piece = lax.dynamic_slice_in_dim(grads, ((parity + shift) % ratio) * half, half, 1)
        perm = []
        for t in range(n_tensor):
            for e in range(n_example):
                target = (e // ratio) * n_example + ratio * t + (e + shift) % ratio
                perm.append((t * n_example + e, target))
        received.append(lax.ppermute(piece, ("tensor", "example"), perm))
    stacked = jnp.stack(received)
    order = (parity - jnp.arange(ratio)) % ratio
    pieces = [lax.dynamic_index_in_dim(stacked, order[p], 0, keepdims=False) for p in range(ratio)]
    return jnp.concatenate(pieces, axis=0)


def body(
    queries, basis_out, basis_in, eigvals, input_fac, grad_fac, cand_slot, score_list, token_count
):
    n_example = lax.axis_size("example")
    n_tensor = lax.axis_size("tensor")
    my_index = lax.axis_index("example")
    cand_total = cand_slot.shape[0]
    token_len = input_fac.shape[1]
    list_len = score_list.shape[1]
    query_total, rows, width = queries.shape
    acts = input_fac.reshape(-1, width)
    grads = grad_fac.reshape(-1, width)
    tokens = acts.shape[0]

    moved_grads = regroup_grads(grads, n_tensor, n_example)
    out_rows = lax.all_gather(basis_out, "tensor", axis=0)
    in_rows = gather_blocks(basis_in, n_example)
    left = jnp.concatenate([queries.reshape(-1, width), acts], axis=0)
    left, moved_grads = lax.optimization_barrier((left, moved_grads))
    half_rotated = line_product(left, in_rows, n_tensor)
    split = query_total * rows
    acts_rot = lax.all_gather(half_rotated[split:], "example", axis=0, tiled=True)
    parts = [half_rotated[q * rows : (q + 1) * rows].T for q in range(query_total)]
    right = jnp.concatenate(parts + [moved_grads], axis=0)
    wide = half_rotated.shape[1]
    core, grads_rot = halving_product(right, out_rows, n_example, query_total * wide)
    grads_rot = grads_rot.reshape(-1, core.shape[1])
    partial = []
    for q in range(query_total):
        scaled = (core[q * wide : (q + 1) * wide].astype(F32) / eigvals).astype(BF)
        weighted = jnp.einsum("tk,lk->tl", grads_rot, scaled, preferred_element_type=F32)
        partial.append(jnp.sum(weighted * acts_rot.astype(F32), axis=1))
    summed = total_over_devices(jnp.stack(partial), n_tensor, n_example)
    by_slot = summed.reshape(query_total, cand_total, token_len)

    my_list = lax.dynamic_index_in_dim(score_list, my_index, 0, keepdims=False)
    ids = jnp.arange(cand_total, dtype=jnp.int32)
    matches = my_list[:, None] == ids[None, :]
    my_slot = jnp.sum(jnp.where(matches, cand_slot[None, :], 0), axis=1)
    my_count = jnp.sum(jnp.where(matches, token_count[None, :], 0), axis=1)
    pick = my_slot[:, None] == ids[None, :]
    scores = jnp.sum(jnp.where(pick[None, :, :, None], by_slot[:, None], F32(0.0)), axis=2)
    live = jnp.arange(token_len, dtype=jnp.int32)[None, :] < my_count[:, None]
    return jnp.where(live[None], scores, F32(0.0))


def solution(mesh):
    in_specs = (
        P(None, "example", "tensor"),
        P("example", "tensor"),
        P("tensor", "example"),
        P("tensor", "example"),
        P("example", None, "tensor"),
        P("example", None, "tensor"),
        P(),
        P(),
        P(),
    )
    out_specs = P(None, "example", None)
    return jax.shard_map(body, mesh=mesh, in_specs=in_specs, out_specs=out_specs, check_vma=False)
```
